128 devices in a mesh: row: 8 (over y, core), col: 16 (over z, x).
Axes of the slice: x: 4, y: 4, z: 4, core: 2. Of those that a mesh axis runs over, the one named last changes fastest.
Arguments:
- features: float32 [16384, 512], P('row'), may hold values from -6 to 6
- jitter: float32 [16384], P('row'), may hold values from 0.25 to 2
Outputs:
- lower: float32 [16384, 2048], P('row', 'col')
- ahead: float32 [16384, 2048], P('row', 'col')
The draws below stay inside these ranges and needn't reach their ends.
All inputs are finite; a program needn't handle non-finite values.
Results may differ from the reference program's by a relative error of at most 0.0003.
Values sent between devices are 32-bit elements; how exact they have to be, the bound alone decides.
No kernel may reach another device: no remote copies, remote signals or barrier semaphores. Data moves between devices by JAX's collectives and lax.ppermute only.
A program may use at most 256 MiB of HBM per device.

```python
import math
import jax
import jax.numpy as jnp
from jax import lax

FEAT = 512
PANEL = 2048
ROWS = 16384
N_ROW = 8


def block_scale(own_key, extent, pieces, low, largest):
    def one(position, parts):
        draws = jax.random.uniform(jax.random.fold_in(jax.random.fold_in(own_key, 6), position), (parts,), jnp.float32, low / len(pieces), largest / len(pieces))
        return jnp.repeat(jnp.exp(draws), extent[position] // parts).reshape((-1,) + (1,) * (len(extent) - position - 1))

    level = one(*pieces[0])
    for cut in pieces[1:]:
        level = level * one(*cut)
    return level


def bell_draw(own_key, extent, deviation, limit, cuts=(), kind=jnp.bfloat16):
    entries = jax.random.normal(own_key, extent, jnp.float32) * deviation
    if len(cuts) > 0:
        entries = block_scale(own_key, extent, cuts, -0.22, 0.18) * entries
    return jnp.clip(entries, min=-limit, max=limit).astype(kind)


def setup_inputs(seed: int = 0) -> dict:
    key_of = jax.random.split(jax.random.key(seed), 3)
    return {
        "features": bell_draw(key_of[0], (ROWS, FEAT), 1.0, 6.0, ((0, 8),), jnp.float32),
        "jitter": jnp.clip(jnp.exp(math.log(2.0) - 2.0794415 * jax.random.uniform(key_of[1], (ROWS,), jnp.float32) ** block_scale(key_of[1], (ROWS,), ((0, 8),), -0.2, 0.2)), 0.25, 2.0),
    }


def kernel_block(left_rows, right_rows):
    products = jnp.dot(left_rows.astype(jnp.float32), right_rows.T.astype(jnp.float32), precision=lax.Precision.HIGHEST, preferred_element_type=jnp.float32)
    left_square = jnp.sum(left_rows * left_rows, axis=1)
    right_square = jnp.sum(right_rows * right_rows, axis=1)
    distance = left_square[:, None] + right_square[None, :] - 2.0 * products
    return jnp.exp(-distance / left_rows.shape[1])

def reference(features, jitter):
    row_count = features.shape[0]
    band_rows = PANEL // N_ROW
    blocks = row_count // (N_ROW * band_rows)

    def to_matrix(values):
        depth = values.shape[1]
        return values.reshape(N_ROW, blocks, band_rows, depth).transpose(1, 0, 2, 3).reshape(row_count, depth)

    def to_stored(values):
        depth = values.shape[1]
        return values.reshape(blocks, N_ROW, band_rows, depth).transpose(1, 0, 2, 3).reshape(row_count, depth)
    ordered = to_matrix(features)
    order_jitter = to_matrix(jitter[:, None])[:, 0]
    panel_feats = ordered[:PANEL]
    rest_rows = ordered[PANEL:]
    diag_mask = lax.broadcasted_iota(jnp.int32, (PANEL, PANEL), 0) == lax.broadcasted_iota(jnp.int32, (PANEL, PANEL), 1)
    diag_block = jnp.where(diag_mask, 1.0 + order_jitter[:PANEL][:, None], kernel_block(panel_feats, panel_feats))
    factor = jnp.linalg.cholesky(diag_block)
    rest_tile = kernel_block(rest_rows, panel_feats)
    lower_rest = lax.linalg.triangular_solve(factor, rest_tile, left_side=False, lower=True, transpose_a=True)
    ahead_tile = kernel_block(rest_rows, ordered[PANEL:2 * PANEL])
    rest_count = row_count - PANEL
    rest_mask = lax.broadcasted_iota(jnp.int32, (rest_count, PANEL), 0) == lax.broadcasted_iota(jnp.int32, (rest_count, PANEL), 1)
    ahead_tile = jnp.where(rest_mask, 1.0 + order_jitter[PANEL:][:, None], ahead_tile)
    ahead_rest = ahead_tile - jnp.dot(lower_rest.astype(jnp.float32), lower_rest[:PANEL].T.astype(jnp.float32), precision=lax.Precision.HIGHEST, preferred_element_type=jnp.float32)
    lower_full = jnp.concatenate([factor, lower_rest], axis=0)
    ahead_full = jnp.concatenate([jnp.zeros((PANEL, PANEL), jnp.float32), ahead_rest], axis=0)
    return (to_stored(lower_full), to_stored(ahead_full))
```

```python
import functools

import jax
import jax.numpy as jnp
from jax import lax
from jax.experimental import pallas as pl
from jax.experimental.pallas import tpu as pltpu
from jax.sharding import PartitionSpec as P

PANEL = 2048
F32 = jnp.float32
BF16 = jnp.bfloat16
NN = (((1,), (0,)), ((), ()))
NT = (((1,), (1,)), ((), ()))
TN = (((0,), (0,)), ((), ()))
MICRO = 32
TILE = 256


def split(x):
    high = x.astype(BF16)
    return high, (x - high.astype(F32)).astype(BF16)


def product(left, right, dims):
    (lc,), (rc,) = dims[0]
    lh, ll = left
    rh, rl = right
    return lax.dot_general(
        jnp.concatenate([lh, ll, lh], lc),
        jnp.concatenate([rh, rh, rl], rc),
        dims,
        preferred_element_type=F32,
    )


def lanes(v, q):
    return jnp.broadcast_to(v[:, q : q + 1], (8, 128))


def sublanes(v, s):
    return jnp.broadcast_to(v[s : s + 1, :], (8, 128))


def micro_rows(work, base, size):
    groups = size // 8
    left = [work[base + 8 * i : base + 8 * i + 8, 0:128] for i in range(groups)]
    right = [work[base + 8 * i : base + 8 * i + 8, 128:256] for i in range(groups)]
    cols = [[lanes(left[i], base + q) for q in range(8 * i + 8)] for i in range(groups)]
    sub = lax.broadcasted_iota(jnp.int32, (8, 128), 0)
    for k in range(size):
        ik, sk = k // 8, k % 8
        inverse = 1.0 / sublanes(cols[ik][k], sk)
        row_left, row_right = sublanes(left[ik], sk), sublanes(right[ik], sk)
        scaled = {q: sublanes(cols[q // 8][k], q % 8) * inverse for q in range(k + 1, size)}
        for i in range(ik, groups):
            raw = cols[i][k]
            if i == ik:
                if sk == 7:
                    continue
                raw = jnp.where(sub > sk, raw, 0.0)
            factor = raw * inverse
            left[i] = left[i] - factor * row_left
            right[i] = right[i] - factor * row_right
            for q in range(k + 1, 8 * i + 8):
                cols[i][q] = cols[i][q] - raw * scaled[q]
    out = []
    for i in range(groups):
        pivots = cols[i][8 * i]
        for s in range(1, 8):
            pivots = jnp.where(sub == s, cols[i][8 * i + s], pivots)
        scale = lax.rsqrt(pivots)
        out.append(jnp.concatenate([left[i] * scale, right[i] * scale], 1))
    return jnp.concatenate(out, 0)


def factor_128(work, block):
    r = lax.broadcasted_iota(jnp.int32, (128, 128), 0)
    c = lax.broadcasted_iota(jnp.int32, (128, 128), 1)
    work[:, 0:128] = block
    work[:, 128:256] = jnp.where(r == c, 1.0, 0.0)
    for base in range(0, 128, MICRO):
        rows = micro_rows(work, base, MICRO)
        work[base : base + MICRO, :] = rows
        if base + MICRO < 128:
            high, low = split(rows)
            update = product((high[:, :128], low[:, :128]), (high, low), TN)
            work[base + MICRO :, :] = work[base + MICRO :, :] - update[base + MICRO :, :]
    lower = jnp.where(r >= c, work[:, 0:128].T, 0.0)
    inverse = jnp.where(r >= c, work[:, 128:256], 0.0)
    return lower, inverse


def factor_kernel(pos, a_in, top_ref, y_ref, a, inv, parts, work, rhs, sem):
    copy = pltpu.make_async_copy(a_in, a, sem)
    copy.start()
    copy.wait()
    tiles = PANEL // TILE
    row_id, col_id = pos[0], pos[1]

    def at(i):
        return pl.ds(pl.multiple_of(i * TILE, TILE), TILE)

    def outer(j, carry):
        o = j * TILE
        here = at(j)
        first = pl.ds(pl.multiple_of(o, 128), 128)
        second = pl.ds(pl.multiple_of(o + 128, 128), 128)
        l11, x11 = factor_128(work, a[first, first])
        x11s = split(x11)
        l21 = product(split(a[second, first]), x11s, NT)
        l21s = split(l21)
        d22 = a[second, second] - product(l21s, l21s, NT)
        l22, x22 = factor_128(work, d22)
        x21 = -product(split(x22), split(product(l21s, x11s, NN)), NN)
        zero = jnp.zeros((128, 128), F32)
        a[first, here] = jnp.concatenate([l11, zero], 1)
        a[second, here] = jnp.concatenate([l21, l22], 1)
        xj = jnp.concatenate([jnp.concatenate([x11, zero], 1), jnp.concatenate([x21, x22], 1)], 0)
        inv[j] = xj
        xjs = split(xj)

        def panel(i, carry):
            p = product(split(a[at(i), here]), xjs, NT)
            a[at(i), here] = p
            high, low = split(p)
            parts[at(i), 0:TILE] = high
            parts[at(i), TILE : 2 * TILE] = low
            return carry

        lax.fori_loop(j + 1, tiles, panel, 0)
        extra = pl.ds(PANEL, 128)
        p = product(split(a[extra, here]), xjs, NT)
        a[extra, here] = p
        ps = split(p)

        def columns(t, carry):
            right = (parts[at(t), 0:TILE], parts[at(t), TILE : 2 * TILE])

            def rows(i, carry):
                left = (parts[at(i), 0:TILE], parts[at(i), TILE : 2 * TILE])
                a[at(i), at(t)] = a[at(i), at(t)] - product(left, right, NT)
                return carry

            lax.fori_loop(t, tiles, rows, 0)
            a[extra, at(t)] = a[extra, at(t)] - product(ps, right, NT)
            return carry

        lax.fori_loop(j + 1, tiles, columns, 0)
        return carry

    lax.fori_loop(0, tiles, outer, 0)
    r = lax.broadcasted_iota(jnp.int32, (128, PANEL), 0)
    c = lax.broadcasted_iota(jnp.int32, (128, PANEL), 1)
    rhs[0:128, :] = jnp.where(c == r + col_id * 128, 1.0, 0.0)
    rhs[128:256, :] = a[PANEL : PANEL + 128, :]

    def back(step, carry):
        j = tiles - 1 - step
        here = at(j)
        y = product(split(rhs[:, here]), split(inv[j]), NN)
        y_ref[:, here] = y
        ys = split(y)

        def earlier(back_by, carry):
            t = j - 1 - back_by
            rhs[:, at(t)] = rhs[:, at(t)] - product(ys, split(a[here, at(t)]), NN)
            return carry

        lax.fori_loop(0, j, earlier, 0)
        return carry

    lax.fori_loop(0, tiles, back, 0)
    rr = pl.ds(pl.multiple_of(row_id * TILE, TILE), TILE)
    cc = pl.ds(pl.multiple_of(col_id * 128, 128), 128)
    gr = lax.broadcasted_iota(jnp.int32, (TILE, 128), 0) + row_id * TILE
    gc = lax.broadcasted_iota(jnp.int32, (TILE, 128), 1) + col_id * 128
    top_ref[...] = jnp.where(gr >= gc, a[rr, cc], 0.0)


def factor_panel(position, system):
    return pl.pallas_call(
        factor_kernel,
        out_shape=[jax.ShapeDtypeStruct((TILE, 128), F32), jax.ShapeDtypeStruct((256, PANEL), F32)],
        in_specs=[pl.BlockSpec(memory_space=pltpu.SMEM), pl.BlockSpec(memory_space=pl.ANY)],
        out_specs=[pl.BlockSpec(memory_space=pltpu.VMEM)] * 2,
        scratch_shapes=[
            pltpu.VMEM((PANEL + 128, PANEL), F32),
            pltpu.VMEM((PANEL // TILE, TILE, TILE), F32),
            pltpu.VMEM((PANEL, 2 * TILE), BF16),
            pltpu.VMEM((128, 256), F32),
            pltpu.VMEM((256, PANEL), F32),
            pltpu.SemaphoreType.DMA,
        ],
        name="factor_panel",
    )(position, system)


def kernel_block(left_rows, right_rows):
    products = jnp.dot(
        left_rows, right_rows.T, precision=lax.Precision.HIGH, preferred_element_type=jnp.float32
    )
    left_square = jnp.sum(left_rows * left_rows, axis=1)
    right_square = jnp.sum(right_rows * right_rows, axis=1)
    distance = left_square[:, None] + right_square[None, :] - 2.0 * products
    return jnp.exp(-distance / left_rows.shape[1])


def local(features, jitter):
    n_rowdev = lax.axis_size("row")
    n_coldev = lax.axis_size("col")
    local_rows, feat = features.shape
    band_rows = PANEL // n_rowdev
    slab_cols = PANEL // n_coldev
    below_count = local_rows - band_rows
    row_id = lax.axis_index("row")
    col_id = lax.axis_index("col")
    own_jitter = jnp.pad(jitter[:band_rows][None, :], ((0, 7), (0, feat - band_rows)))
    gathered = lax.all_gather(jnp.concatenate([features[:band_rows], own_jitter], 0), "row", axis=0)
    panel_feats = gathered[:, :band_rows].reshape(PANEL, feat)
    panel_jitter = gathered[:, band_rows, :band_rows].reshape(PANEL)
    share = band_rows // slab_cols
    sends = []
    for c in range(n_coldev):
        for r in range(n_rowdev):
            source_col = (c % share) * n_rowdev + r
            sends.append(((c // share) * n_coldev + source_col, r * n_coldev + c))
    ahead_piece = lax.dynamic_slice_in_dim(
        features, band_rows + (col_id // n_rowdev) * slab_cols, slab_cols, 0
    )
    ahead_feats = lax.ppermute(ahead_piece, ("row", "col"), sends)
    system = kernel_block(jnp.concatenate([panel_feats, ahead_feats], 0), panel_feats)
    r = lax.broadcasted_iota(jnp.int32, system.shape, 0)
    c = lax.broadcasted_iota(jnp.int32, system.shape, 1)
    system = jnp.where(r == c, 1.0 + panel_jitter[None, :], system)
    position = jnp.stack([row_id, col_id]).astype(jnp.int32)
    top_rows, solve = factor_panel(position, system)

    below_feats = features[band_rows:]
    below = kernel_block(below_feats, panel_feats)
    ahead_tile = kernel_block(below_feats, ahead_feats)
    row_pos = lax.broadcasted_iota(jnp.int32, (below_count, slab_cols), 0)
    col_pos = lax.broadcasted_iota(jnp.int32, (below_count, slab_cols), 1)
    match_mask = (row_pos < band_rows) & (
        row_id * band_rows + row_pos == col_id * slab_cols + col_pos
    )
    ahead_tile = jnp.where(match_mask, 1.0 + jitter[band_rows:][:, None], ahead_tile)
    both = jnp.dot(below, solve.T, precision=lax.Precision.HIGH, preferred_element_type=jnp.float32)
    lower_out = jnp.concatenate([top_rows, both[:, :slab_cols]], axis=0)
    ahead_out = jnp.concatenate(
        [jnp.zeros((band_rows, slab_cols), jnp.float32), ahead_tile - both[:, slab_cols:]], axis=0
    )
    return (lower_out, ahead_out)


def solution(mesh):
    return jax.shard_map(
        local,
        mesh=mesh,
        in_specs=(P("row", None), P("row")),
        out_specs=(P("row", "col"), P("row", "col")),
        check_vma=False,
    )
```
